32 devices in a mesh: exp: 4 (over x, core), seq: 8 (over z, y).
Axes of the slice: x: 2, y: 2, z: 4, core: 2. Of those that a mesh axis runs over, the one named last changes fastest.
Arguments:
- hidden_in: bfloat16 [2048, 4096], P(('exp', 'seq')), may hold values from -3 to 3
- doc_ids: int32 [2048], P(('exp', 'seq')), may hold values from 0 to 31, never falling along the last dimension, each value on 1 to 256 neighbouring positions
- attn_gain: float32 [4096], replicated, may hold values from 0.1 to 1.9
- q_weight: bfloat16 [4096, 4096], P('exp', 'seq'), may hold values from -0.09375 to 0.09375
- kv_weight: bfloat16 [4, 4096, 256], P(None, 'exp'), may hold values from -0.09375 to 0.09375
- q_gain: float32 [128], replicated, may hold values from 0.5 to 5, as said below
- k_gain: float32 [128], replicated, may hold values from 0.5 to 5, as said below
- out_weight: bfloat16 [4096, 4096], P('seq', 'exp'), may hold values from -0.25 to 0.25
- ffn_gain: float32 [4096], replicated, may hold values from 0.1 to 1.9
- router_weight: bfloat16 [4096, 32], replicated, may hold values from -0.0234375 to 0.0234375
- routes: int32 [2048, 8], P(('exp', 'seq')), may hold values from 0 to 31, all different within a row; in each aligned block of 64 rows (0 to 63, 64 to 127, ...) at most 32 rows name the same one
- expert_in: bfloat16 [32, 4096, 1536], P(('exp', 'seq')), may hold values from -0.09375 to 0.09375
- expert_out: bfloat16 [32, 768, 4096], P(('exp', 'seq')), may hold values from -0.875 to 0.875
Outputs:
- layer_out: bfloat16 [2048, 4096], P(('exp', 'seq'))
The draws below stay inside these ranges and needn't reach their ends.
Inputs may be any that keep to these rules, and one draw needn't show every extreme that they name: `routes`: each row names 8 different experts. Among the rows of one device no expert is named by more than 32 rows, a bound that some block reaches. `doc_ids`: never falls along the tokens; each document has 1 to 256 tokens, one has exactly 256. `q_gain`: Positive. `k_gain`: Positive.
All inputs are finite; a program needn't handle non-finite values.
Results may differ from the reference program's by a relative error of at most 0.019.
The reference program's roundings to bfloat16 on the way count: a program that leaves them out, or rounds other values in their place, can miss the bound.
Values may be sent and summed in bfloat16 or wider, within the bound.
No kernel may reach another device: no remote copies, remote signals or barrier semaphores. Data moves between devices by JAX's collectives and lax.ppermute only.
A program may use at most 128 MiB of HBM per device.

```python
import math
import jax
import jax.numpy as jnp
import numpy as np
from jax import lax

D = 4096
HEADS = 32
KV = 4
HD = 128
TOPK = 8
FFE = 768
TOK_DEV = 64
DOCS = 8
EXPERTS = 32
CAP = 32
SEQLEN = 512
TOKENS = 2048
MOST_DOC = 256
N_EXP = 4
N_SEQ = 8


def draw_q_gain(key, part):
    key = jax.random.fold_in(key, 11)
    return jnp.exp(jax.random.uniform(key, (HD,), jnp.float32, -0.69, 0.69))


def draw_k_gain(key, part):
    key = jax.random.fold_in(key, 23)
    return jnp.exp(jax.random.uniform(key, (HD,), jnp.float32, -0.69, 0.69))


def steps_of(rng, shape, cuts, low, top_value):
    level, own = 1.0, jax.random.fold_in(rng, 6)
    for dim, shards_of in cuts:
        steps = jnp.exp(jax.random.uniform(jax.random.fold_in(own, dim), (shards_of,), jnp.float32, low / len(cuts), top_value / len(cuts)))
        level = level * jnp.repeat(steps, shape[dim] // shards_of).reshape([-1 if axis == dim else 1 for axis in range(len(shape))])
    return level


def length_profile(amount, total, bound, lean):
    weights = [(1 << 20) // math.isqrt(grade ** lean) + 1 for grade in range(2, amount + 1)]
    rest, given = total - bound - (amount - 1), [1] * (amount - 1)
    while rest > 0:
        free = [i for i in range(amount - 1) if given[i] < bound]
        whole, remaining = sum([weights[i] for i in free]), rest
        for i in free:
            addition = min(bound - given[i], max(1, remaining * weights[i] // whole), rest)
            given[i] = given[i] + addition
            rest = rest - addition
    return np.array([bound] + given)


def ragged_sizes(own_key, number_of, total, limit, lean):
    if number_of == 2:
        one = jax.random.randint(own_key, (), max(1, total - limit), min(limit, total - 1) + 1)
        return jnp.stack([one, total - one])
    lengths = jnp.asarray(length_profile(number_of, total, limit, lean), jnp.int32)
    twos = (number_of - 1) // 2
    giver, taker = lengths[1:1 + 2 * twos:2], lengths[2:2 + 2 * twos:2]
    margin = jnp.minimum(giver - 1, limit - taker)
    passed = jax.random.randint(jax.random.fold_in(own_key, 1), (twos,), 0, 1 << 20) % (margin + 1)
    lengths = lengths.at[1:1 + 2 * twos:2].set(giver - passed).at[2:2 + 2 * twos:2].set(taker + passed)
    return lengths[jax.random.permutation(jax.random.fold_in(own_key, 2), number_of)]


def deal_out(stream_key, own, number, rows, number_of, top, reach, lean):
    order = jax.random.permutation(stream_key, number_of)
    heavy_load, common = load_shares(number_of, rows * top, reach, lean, True), load_shares(number_of, rows * top, reach, lean, False)
    places = jnp.arange(number_of)

    def named(sizes, rotation):
        used = int((sizes > 0).sum())
        fixed = max(1, used // 4)
        moved = fixed + (places - fixed + rotation * (used - fixed)) % max(1, number_of - fixed)
        return jnp.zeros((number_of,), jnp.int32).at[order[jnp.where(places < fixed, places, moved)]].set(jnp.asarray(sizes, jnp.int32))

    sizes = jnp.where(number % 4 == 0, named(heavy_load, number // 4), named(common, number - number // 4 - 1))
    mixed = jax.random.permutation(jax.random.fold_in(own, 3), number_of)
    giver, sink = mixed[0:number_of // 2 * 2:2], mixed[1:number_of // 2 * 2:2]
    slack = jnp.minimum(sizes[giver] - 1, reach - sizes[sink]) // 2
    slack = jnp.where((giver == order[0]) | (sink == order[0]) | (sizes[sink] == 0), 0, jnp.maximum(slack, 0))
    moved = jax.random.randint(jax.random.fold_in(own, 4), (number_of // 2,), 0, 1 << 20) % (slack + 1)
    sizes = sizes.at[giver].add(-moved).at[sink].add(moved)
    items = jnp.searchsorted(jnp.cumsum(sizes), jnp.arange(rows * top), side="right").astype(jnp.int32)
    listing = items.reshape(top, rows).T
    listing = listing[jax.random.permutation(jax.random.fold_in(own, 1), rows)]
    rotation = jax.random.randint(jax.random.fold_in(own, 2), (rows, 1), 0, top)
    return jnp.take_along_axis(listing, (jnp.arange(top)[None, :] + rotation) % top, axis=1)


def load_shares(count, total, reach, lean, full):
    loads = [(1 << 20) // math.isqrt(standing ** lean) + 1 for standing in range(1, count + 1)]
    largest = reach if full else min(reach, max(-(-total // count), total * loads[0] // sum(loads)))
    least = 1 if total - largest >= count - 1 else 0
    given, rest = [largest] + [least] * (count - 1), total - largest - least * (count - 1)
    while rest > 0:
        candidates = [i for i in range(1, count) if given[i] < largest] or [i for i in range(1, count) if given[i] < reach]
        pool, left = sum([loads[i] for i in candidates]), rest
        for i in candidates:
            addition = min(reach - given[i], max(1, left * loads[i] // pool), rest)
            given[i] = given[i] + addition
            rest = rest - addition
    return np.array(given)


def gaussian(rng, dims, deviation, limit, shards=(), kind=jnp.bfloat16):
    array = jax.random.normal(rng, dims, jnp.float32) * deviation
    if len(shards) > 0:
        array = steps_of(rng, dims, shards, -0.22, 0.18) * array
    return jnp.clip(array, min=-limit, max=limit).astype(kind)


def setup_inputs(seed: int = 0) -> dict:
    seeds = jax.random.split(jax.random.key(seed), 14)
    hidden_in = gaussian(seeds[0], (TOKENS, D), 0.5, 3.0, ((0, 32),))
    doc_ids = jnp.searchsorted(jnp.cumsum(ragged_sizes(seeds[1], DOCS * N_EXP, TOKENS, MOST_DOC, 1)), jnp.arange(TOKENS), side="right").astype(jnp.int32)
    attn_gain = jnp.clip(1.0 + 0.18 * jax.random.normal(seeds[2], (D,), jnp.float32), 0.1, 1.9)
    q_weight = gaussian(seeds[3], (D, HEADS * HD), D ** -0.5, 0.09375, ((0, 4), (1, 8)))
    kv_weight = gaussian(seeds[4], (KV, D, 2 * HD), D ** -0.5, 0.09375, ((1, 4),))
    q_gain = draw_q_gain(jax.random.fold_in(seeds[13], 71), 0)
    k_gain = draw_k_gain(jax.random.fold_in(seeds[13], 71), 0)
    out_weight = gaussian(seeds[7], (HEADS * HD, D), (HEADS * HD // 8) ** -0.5, 0.25, ((0, 8), (1, 4)))
    ffn_gain = jnp.clip(1.0 + 0.18 * jax.random.normal(seeds[8], (D,), jnp.float32), 0.1, 1.9)
    router_weight = gaussian(seeds[9], (D, EXPERTS), (16 * D) ** -0.5, 0.0234375)
    routes_keys = jax.random.split(jax.random.fold_in(seeds[10], 1), TOKENS // TOK_DEV)
    routes_turns = jax.random.permutation(jax.random.fold_in(seeds[10], 3), TOKENS // TOK_DEV)
    routes = jax.vmap(lambda own, number: deal_out(jax.random.fold_in(seeds[10], 2), own, number, TOK_DEV, EXPERTS, TOPK, CAP, 2))(routes_keys, routes_turns).reshape((TOKENS, TOPK))
    expert_in = gaussian(seeds[11], (EXPERTS, D, 2 * FFE), D ** -0.5, 0.09375, ((0, 32),))
    expert_out = gaussian(seeds[12], (EXPERTS, FFE, D), (FFE // 16) ** -0.5, 0.875, ((0, 32),))
    return dict(hidden_in=hidden_in, doc_ids=doc_ids, attn_gain=attn_gain, q_weight=q_weight, kv_weight=kv_weight, q_gain=q_gain, k_gain=k_gain, out_weight=out_weight, ffn_gain=ffn_gain, router_weight=router_weight, routes=routes, expert_in=expert_in, expert_out=expert_out)


def rms_scale(values, gain):
    return values * lax.rsqrt(lax.optimization_barrier(jnp.mean(values * values, axis=-1, keepdims=True)) + 1e-06) * gain

def rotate(values, position):
    half = values.shape[-1] // 2
    freq = jnp.exp(-(2.0 * jnp.arange(half, dtype=jnp.float32) / values.shape[-1]) * math.log(1000000.0))
    angle = position[:, None, None] * freq
    cosine = jnp.cos(angle)
    sine = jnp.sin(angle)
    first = values[..., :half]
    second = values[..., half:]
    return jnp.concatenate([first * cosine - second * sine, second * cosine + first * sine], axis=-1)

def attend(queries, keys, values, position, docs):
    length = keys.shape[0]
    block = min(512, length)
    count = length // block
    scale = 1.0 / math.sqrt(keys.shape[-1])
    keys_wide = keys.astype(jnp.float32)
    values_wide = values.astype(jnp.float32)

    def one_block(items):
        query_block, query_pos, query_docs = items
        scores = jnp.einsum('qhd,kd->hqk', query_block.astype(jnp.float32), keys_wide) * scale
        allowed = (position[None, :] <= query_pos[:, None]) & (docs[None, :] == query_docs[:, None])
        scores = jnp.where(allowed[None], scores, -1e+30)
        top = lax.optimization_barrier(jnp.max(scores, axis=-1, keepdims=True))
        expo = jnp.exp(scores - top)
        weights = (expo / lax.optimization_barrier(jnp.sum(expo, axis=-1, keepdims=True))).astype(jnp.bfloat16)
        return jnp.einsum('hqk,kd->qhd', weights.astype(jnp.float32), values_wide).astype(jnp.bfloat16)
    heads = queries.shape[1]
    out = lax.map(one_block, (queries.reshape(count, block, heads, -1), position.reshape(count, block), docs.reshape(count, block)))
    return out.reshape(length, -1)

def reference(hidden_in, doc_ids, attn_gain, q_weight, kv_weight, q_gain, k_gain, out_weight, ffn_gain, router_weight, routes, expert_in, expert_out):
    normed = rms_scale(hidden_in.astype(jnp.float32), attn_gain).astype(jnp.bfloat16)
    position = jnp.arange(SEQLEN, dtype=jnp.float32)
    group = HEADS // KV
    group_width = HEADS // N_SEQ * HD

    def one_sequence(items):
        rows, docs = items
        queries = jnp.dot(rows, q_weight, preferred_element_type=jnp.float32).reshape(SEQLEN, HEADS, HD)
        queries = rotate(rms_scale(queries, q_gain), position).astype(jnp.bfloat16)
        pieces = []
        for head_group in range(KV):
            pairs = jnp.dot(rows, kv_weight[head_group], preferred_element_type=jnp.float32)
            keys = rotate(rms_scale(pairs[:, None, :HD], k_gain), position)[:, 0].astype(jnp.bfloat16)
            values = pairs[:, HD:].astype(jnp.bfloat16)
            pieces.append(attend(queries[:, head_group * group:(head_group + 1) * group], keys, values, position, docs))
        context = jnp.concatenate(pieces, axis=1)
        total = jnp.zeros((SEQLEN, D), jnp.float32)
        for member in range(N_SEQ):
            lower = member * group_width
            partial_value = jnp.dot(context[:, lower:lower + group_width], out_weight[lower:lower + group_width], preferred_element_type=jnp.float32).astype(jnp.bfloat16)
            partial_value = lax.optimization_barrier(partial_value)
            total = total + partial_value.astype(jnp.float32)
        return total
    attn_out = lax.map(one_sequence, (normed.reshape(N_EXP, SEQLEN, D), doc_ids.reshape(N_EXP, SEQLEN)))
    mid = (hidden_in.astype(jnp.float32) + attn_out.reshape(TOKENS, D)).astype(jnp.bfloat16)
    ffn_in = rms_scale(mid.astype(jnp.float32), ffn_gain).astype(jnp.bfloat16)
    logits = jnp.dot(ffn_in, router_weight, preferred_element_type=jnp.float32)
    probs = jax.nn.softmax(logits, axis=-1)
    picked = jnp.take_along_axis(probs, routes, axis=1)
    gates = picked / lax.optimization_barrier(jnp.sum(picked, axis=-1, keepdims=True))
    flat_expert = routes.reshape(-1).astype(jnp.int32)
    picks = flat_expert.shape[0]
    order = jnp.argsort(flat_expert, stable=True).astype(jnp.int32)
    counts = lax.optimization_barrier(jnp.sum((flat_expert[:, None] == jnp.arange(EXPERTS, dtype=jnp.int32)[None, :]).astype(jnp.int32), axis=0))
    starts = jnp.cumsum(counts) - counts
    load = N_EXP * N_SEQ * CAP
    flat_gate = gates.reshape(-1)

    def add_expert(expert, total):
        slot = jnp.arange(load, dtype=jnp.int32)
        where_at = jnp.minimum(starts[expert] + slot, picks - 1).astype(jnp.int32)
        pick = order[where_at]
        token = (pick // TOPK).astype(jnp.int32)
        live = slot < counts[expert]
        rows = ffn_in[token]
        both = jnp.dot(rows, expert_in[expert], preferred_element_type=jnp.float32)
        act = (jax.nn.silu(both[:, :FFE]) * both[:, FFE:]).astype(jnp.bfloat16)
        result = jnp.dot(act, expert_out[expert], preferred_element_type=jnp.float32).astype(jnp.bfloat16)
        term = jnp.where(live[:, None], flat_gate[pick][:, None] * result.astype(jnp.float32), 0.0)
        return total.at[token].add(term)
    mixture = lax.fori_loop(0, EXPERTS, add_expert, jnp.zeros((TOKENS, D), jnp.float32))
    return (mid.astype(jnp.float32) + mixture).astype(jnp.bfloat16)
```

```python
import functools
import math

import jax
import jax.numpy as jnp
from jax import lax
from jax.sharding import PartitionSpec as P

HEADS = 32
KV = 4
HD = 128
TOPK = 8


def rms_scale(values, gain):
    return values * lax.rsqrt(jnp.mean(values * values, axis=-1, keepdims=True) + 1e-06) * gain


def rotate(values, position):
    half = values.shape[-1] // 2
    freq = jnp.exp(
        -(2.0 * jnp.arange(half, dtype=jnp.float32) / values.shape[-1]) * math.log(1000000.0)
    )
    angle = position[:, None, None] * freq
    cosine = jnp.cos(angle)
    sine = jnp.sin(angle)
    first = values[..., :half]
    second = values[..., half:]
    return jnp.concatenate(
        [first * cosine - second * sine, second * cosine + first * sine], axis=-1
    )


def swap(values, axis, size, mask):
    return lax.ppermute(values, axis, [(i, i ^ mask) for i in range(size)])


def permute_blocks(values, own, count):
    width = values.shape[-1]
    bit = count // 2
    span = width // 2
    while bit > 0:
        parts = values.reshape(values.shape[:-1] + (width // (2 * span), 2, span))
        parts = jnp.where((own & bit) != 0, parts[..., ::-1, :], parts)
        values = parts.reshape(values.shape)
        bit //= 2
        span //= 2
    return values


def gather_pieces(shard, axis, size):
    pieces = []
    for far in range(size // 2):
        near = shard if far == 0 else swap(shard, axis, size, 2 * far)
        pieces += [near, swap(near, axis, size, 1)]
    return pieces


def attend(queries, keys, values, query_pos, query_docs, position, docs):
    scale = 1.0 / math.sqrt(keys.shape[-1])
    scores = jnp.einsum("qhd,kd->hqk", queries, keys, preferred_element_type=jnp.float32) * scale
    allowed = (position[None, :] <= query_pos[:, None]) & (docs[None, :] == query_docs[:, None])
    scores = jnp.where(allowed[None], scores, -1e30)
    top = jnp.max(scores, axis=-1, keepdims=True)
    expo = jnp.exp(scores - top)
    weights = (expo / jnp.sum(expo, axis=-1, keepdims=True)).astype(jnp.bfloat16)
    context = jnp.einsum(
        "hqk,kd->qhd", weights, values, preferred_element_type=jnp.float32
    ).astype(jnp.bfloat16)
    return context.reshape(queries.shape[0], -1)


def attention_rows(
    hidden_in, doc_ids, attn_gain, q_weight, kv_weight, q_gain, k_gain, out_weight, n_exp, n_seq
):
    own_exp = lax.axis_index("exp")
    own_seq = lax.axis_index("seq")
    heads_dev = q_weight.shape[1] // HD
    rows = hidden_in.shape[0]
    kv_local = lax.dynamic_index_in_dim(
        kv_weight, own_seq * heads_dev // (HEADS // KV), 0, keepdims=False
    )
    normed = rms_scale(hidden_in.astype(jnp.float32), attn_gain).astype(jnp.bfloat16)
    normed = permute_blocks(normed, own_exp, n_exp)
    blocks = gather_pieces(normed, "seq", n_seq)
    qkv_pieces = gather_pieces(jnp.concatenate([q_weight, kv_local], axis=1), "exp", n_exp)
    out_pieces = gather_pieces(out_weight, "exp", n_exp)
    qkv_full = jnp.concatenate(qkv_pieces, axis=0)
    out_full = jnp.concatenate(out_pieces, axis=1)

    order = own_seq ^ jnp.arange(n_seq, dtype=jnp.int32)
    all_docs = lax.all_gather(doc_ids, "seq", axis=0, tiled=False)
    docs = jnp.take(all_docs, order, axis=0).reshape(-1)
    position = (
        (order[:, None] * rows + jnp.arange(rows, dtype=jnp.int32)[None, :])
        .reshape(-1)
        .astype(jnp.float32)
    )
    q_width = heads_dev * HD
    queries, keys, values = [], [], []
    count = n_seq // 2
    for far in range(count):
        span = slice(2 * far * rows, 2 * (far + 1) * rows)
        tokens = jnp.concatenate(blocks[2 * far : 2 * far + 2], axis=0)
        mixed = jnp.dot(tokens, qkv_full, preferred_element_type=jnp.float32)
        query = mixed[:, :q_width].reshape(2 * rows, heads_dev, HD)
        queries.append(rotate(rms_scale(query, q_gain), position[span]).astype(jnp.bfloat16))
        key = mixed[:, None, q_width : q_width + HD]
        keys.append(rotate(rms_scale(key, k_gain), position[span])[:, 0].astype(jnp.bfloat16))
        values.append(mixed[:, q_width + HD :].astype(jnp.bfloat16))
    keys = jnp.concatenate(keys, axis=0)
    values = jnp.concatenate(values, axis=0)
    total = 0.0
    for far in reversed(range(count)):
        span = slice(2 * far * rows, 2 * (far + 1) * rows)
        context = attend(
            queries[far], keys, values, position[span], docs[span], position, docs
        )
        partial = jnp.dot(context, out_full, preferred_element_type=jnp.float32).astype(
            jnp.bfloat16
        )
        other = swap(partial[rows:], "seq", n_seq, 1)
        pair = partial[:rows].astype(jnp.float32) + other.astype(jnp.float32)
        if far > 0:
            pair = swap(pair.astype(jnp.bfloat16), "seq", n_seq, 2 * far).astype(jnp.float32)
        total = total + pair
    return permute_blocks(total, own_exp, n_exp)


def router_gates(ffn_in, router_weight, routes):
    experts = router_weight.shape[1]
    logits = jnp.dot(ffn_in, router_weight, preferred_element_type=jnp.float32)
    probs = jax.nn.softmax(logits, axis=-1)
    chosen = routes[:, :, None] == jnp.arange(experts, dtype=jnp.int32)[None, None, :]
    return probs, chosen


def experts_gathered(ffn_in, router_weight, routes, expert_in, expert_out, n_exp, n_seq):
    rows, depth = ffn_in.shape
    half = depth // 2
    experts = router_weight.shape[1]
    own_exp = lax.axis_index("exp")
    own_seq = lax.axis_index("seq")
    in_weights = [expert_in[0], swap(expert_in[0], "exp", n_exp, 1)]
    out_weights = [expert_out[0], swap(expert_out[0], "exp", n_exp, 1)]
    width = expert_out.shape[1]
    ids = [(own_exp ^ m) * n_seq + own_seq for m in range(2)]

    probs, chosen = router_gates(ffn_in, router_weight, routes)
    picked = jnp.where(jnp.any(chosen, axis=1), probs, 0.0)
    gates = picked / jnp.sum(picked, axis=-1, keepdims=True)
    gate_high = gates.astype(jnp.bfloat16)
    gate_low = (gates - gate_high.astype(jnp.float32)).astype(jnp.bfloat16)
    extra = jnp.concatenate([gate_high, gate_low], axis=1)
    extra = jnp.pad(extra, ((0, 0), (0, -extra.shape[1] % 128)))
    first = jnp.concatenate([ffn_in[:, :half], extra], axis=1)
    second = ffn_in[:, half:]

    def along_x(values):
        return swap(values, "exp", n_exp, 2)

    def along_y(values):
        return swap(values, "seq", n_seq, 1)

    total = 0.0
    for far in range(n_seq // 2):
        a0 = first if far == 0 else swap(first, "seq", n_seq, 2 * far)
        b0 = second if far == 0 else swap(second, "seq", n_seq, 2 * far)
        ax, ay, bx, by = along_x(a0), along_y(a0), along_x(b0), along_y(b0)
        axy, bxy = along_y(ax), along_x(by)
        left = jnp.concatenate([a0, ax, ay, axy], axis=0)
        right = jnp.concatenate([b0, bx, by, bxy], axis=0)
        tokens = jnp.concatenate([left[:, :half], right], axis=1)
        table = left[:, half:].astype(jnp.float32)
        lanes = jnp.arange(table.shape[1], dtype=jnp.int32)[None, :]
        partial = 0.0
        for m in range(2):
            mine = (lanes == ids[m]) | (lanes == ids[m] + experts)
            gate = jnp.sum(jnp.where(mine, table, 0.0), axis=1, keepdims=True)
            both = jnp.dot(tokens, in_weights[m], preferred_element_type=jnp.float32)
            act = (jax.nn.silu(both[:, :width]) * both[:, width:] * gate).astype(jnp.bfloat16)
            partial = partial + jnp.dot(act, out_weights[m], preferred_element_type=jnp.float32)
        partial = partial.astype(jnp.bfloat16)

        def added(kept, sent, along):
            return (kept.astype(jnp.float32) + along(sent).astype(jnp.float32)).astype(
                jnp.bfloat16
            )

        pa = partial[:, :half]
        pb = partial[:, half:]
        pa = added(pa[: 2 * rows], pa[2 * rows :], along_y)
        pa = added(pa[:rows], pa[rows:], along_x)
        near = jnp.concatenate([pb[:rows], pb[2 * rows : 3 * rows]], axis=0)
        away = jnp.concatenate([pb[rows : 2 * rows], pb[3 * rows :]], axis=0)
        pb = added(near, away, along_x)
        pb = added(pb[:rows], pb[rows:], along_y)
        if far > 0:
            pa = swap(pa, "seq", n_seq, 2 * far)
            pb = swap(pb, "seq", n_seq, 2 * far)
        total = total + jnp.concatenate([pa, pb], axis=1).astype(jnp.float32)
    return total


def experts_exchanged(ffn_in, router_weight, routes, expert_in, expert_out):
    tok_count = ffn_in.shape[0]
    experts = router_weight.shape[1]
    capacity = 2 * tok_count * TOPK // experts
    probs, chosen = router_gates(ffn_in, router_weight, routes)
    picked = jnp.sum(jnp.where(chosen, probs[:, None, :], 0.0), axis=-1)
    gates = picked / jnp.sum(picked, axis=-1, keepdims=True)
    flat_hot = chosen.reshape(tok_count * TOPK, experts).astype(jnp.int32)
    before = jnp.cumsum(flat_hot, axis=0) - flat_hot
    slots = jnp.sum(before * flat_hot, axis=-1).reshape(tok_count, TOPK)
    slot_hot = slots[:, :, None] == jnp.arange(capacity, dtype=jnp.int32)[None, None, :]
    placing = jnp.sum(
        (chosen[:, :, :, None] & slot_hot[:, :, None, :]).astype(jnp.bfloat16), axis=1
    )
    sending = jnp.einsum("tec,td->ecd", placing, ffn_in, preferred_element_type=jnp.float32).astype(
        jnp.bfloat16
    )
    received = lax.all_to_all(sending, ("exp", "seq"), split_axis=0, concat_axis=0, tiled=True)
    flat = received.reshape(-1, received.shape[-1])
    both = jnp.dot(flat, expert_in[0], preferred_element_type=jnp.float32)
    width = expert_out.shape[1]
    act = (jax.nn.silu(both[:, :width]) * both[:, width:]).astype(jnp.bfloat16)
    result = jnp.dot(act, expert_out[0], preferred_element_type=jnp.float32).astype(jnp.bfloat16)
    returned = lax.all_to_all(
        result.reshape(received.shape), ("exp", "seq"), split_axis=0, concat_axis=0, tiled=True
    )
    index = (routes * capacity + slots).reshape(-1)
    rows = jnp.take(returned.reshape(experts * capacity, -1), index, axis=0).reshape(
        tok_count, TOPK, -1
    )
    mixture = jnp.einsum("tk,tkd->td", gates, rows.astype(jnp.float32))
    return mixture


def local(
    hidden_in,
    doc_ids,
    attn_gain,
    q_weight,
    kv_weight,
    q_gain,
    k_gain,
    out_weight,
    ffn_gain,
    router_weight,
    routes,
    expert_in,
    expert_out,
    *,
    n_exp,
    n_seq,
):
    attn_rows = attention_rows(
        hidden_in, doc_ids, attn_gain, q_weight, kv_weight, q_gain, k_gain, out_weight, n_exp, n_seq
    )
    mid = (hidden_in.astype(jnp.float32) + attn_rows).astype(jnp.bfloat16)
    ffn_in = rms_scale(mid.astype(jnp.float32), ffn_gain).astype(jnp.bfloat16)
    tok_count = hidden_in.shape[0]
    capacity = 2 * tok_count * TOPK // router_weight.shape[1]
    if n_exp == 4 and 2 * capacity >= tok_count:
        mixture = experts_gathered(
            ffn_in, router_weight, routes, expert_in, expert_out, n_exp, n_seq
        )
    else:
        mixture = experts_exchanged(ffn_in, router_weight, routes, expert_in, expert_out)
    return (mid.astype(jnp.float32) + mixture).astype(jnp.bfloat16)


def solution(mesh):
    in_specs = (
        P(("exp", "seq"), None),
        P(("exp", "seq")),
        P(),
        P("exp", "seq"),
        P(None, "exp", None),
        P(),
        P(),
        P("seq", "exp"),
        P(),
        P(),
        P(("exp", "seq"), None),
        P(("exp", "seq"), None, None),
        P(("exp", "seq"), None, None),
    )
    out_specs = P(("exp", "seq"), None)
    body = functools.partial(local, n_exp=mesh.shape["exp"], n_seq=mesh.shape["seq"])
    return jax.shard_map(body, mesh=mesh, in_specs=in_specs, out_specs=out_specs, check_vma=False)
```

```python
import functools
import math

import jax
import jax.numpy as jnp
from jax import lax
from jax.sharding import PartitionSpec as P

HEADS = 32
KV = 4
HD = 128
TOPK = 8


def rms_scale(values, gain):
    return values * lax.rsqrt(jnp.mean(values * values, axis=-1, keepdims=True) + 1e-06) * gain


def rotate(values, position):
    half = values.shape[-1] // 2
    freq = jnp.exp(
        -(2.0 * jnp.arange(half, dtype=jnp.float32) / values.shape[-1]) * math.log(1000000.0)
    )
    angle = position[:, None, None] * freq
    cosine = jnp.cos(angle)
    sine = jnp.sin(angle)
    first = values[..., :half]
    second = values[..., half:]
    return jnp.concatenate(
        [first * cosine - second * sine, second * cosine + first * sine], axis=-1
    )


class Link:
    def __init__(self, axis, size, depth=1):
        self.axis, self.size, self.depth = axis, size, depth
        self.results = []

    def send(self, values, mask, after=()):
        waits = self.results[-self.depth :][:1] if len(self.results) >= self.depth else []
        waits = tuple(waits) + tuple(after)
        if waits:
            values = lax.optimization_barrier((values, waits))[0]
        result = lax.ppermute(values, self.axis, [(i, i ^ mask) for i in range(self.size)])
        self.results.append(result)
        return result


def attend(queries, keys, values, position, docs):
    scale = 1.0 / math.sqrt(keys.shape[-1])
    scores = jnp.einsum("qhd,kd->hqk", queries, keys, preferred_element_type=jnp.float32) * scale
    allowed = (position[None, :] <= position[:, None]) & (docs[None, :] == docs[:, None])
    scores = jnp.where(allowed[None], scores, -1e30)
    top = jnp.max(scores, axis=-1, keepdims=True)
    expo = jnp.exp(scores - top)
    weights = (expo / jnp.sum(expo, axis=-1, keepdims=True)).astype(jnp.bfloat16)
    context = jnp.einsum(
        "hqk,kd->qhd", weights, values, preferred_element_type=jnp.float32
    ).astype(jnp.bfloat16)
    return context.reshape(queries.shape[0], -1)


def attention_rows(
    hidden_in, doc_ids, attn_gain, q_weight, kv_weight, q_gain, k_gain, out_weight, links
):
    x_link, core_link, y_link, z_link = links
    n_exp, n_seq = x_link.size, y_link.size
    own_exp = lax.axis_index("exp")
    own_seq = lax.axis_index("seq")
    heads_dev = q_weight.shape[1] // HD
    rows, depth = hidden_in.shape
    count = n_seq // 2
    normed = rms_scale(hidden_in.astype(jnp.float32), attn_gain).astype(jnp.bfloat16)
    tagged = jnp.concatenate(
        [normed, jnp.broadcast_to(doc_ids.astype(jnp.bfloat16)[:, None], (rows, 128))], axis=1
    )
    planes = [tagged]
    mirrored = [y_link.send(tagged, 1)]
    for far in range(1, count):
        planes.append(z_link.send(tagged, 2 * far))
    kv_local = lax.dynamic_index_in_dim(
        kv_weight, own_seq * heads_dev // (HEADS // KV), 0, keepdims=False
    )
    qkv_shard = jnp.concatenate([q_weight, kv_local], axis=1)
    qkv_pieces, out_pieces = [], []
    for shard, pieces in ((qkv_shard, qkv_pieces), (out_weight, out_pieces)):
        for far in range(n_exp // 2):
            near = shard if far == 0 else x_link.send(shard, 2 * far)
            pieces += [near, core_link.send(near, 1)]
    for far in range(1, count):
        mirrored.append(y_link.send(planes[far], 1))
    span = q_weight.shape[0]
    qkv_full = jnp.zeros((depth, qkv_shard.shape[1]), jnp.bfloat16)
    out_full = jnp.zeros((out_weight.shape[0], depth), jnp.bfloat16)
    for m in range(n_exp):
        start = (own_exp ^ m) * span
        qkv_full = lax.dynamic_update_slice(qkv_full, qkv_pieces[m], (start, 0))
        out_full = lax.dynamic_update_slice(out_full, out_pieces[m], (0, start))

    order = own_seq ^ jnp.arange(n_seq, dtype=jnp.int32)
    position = (
        (order[:, None] * rows + jnp.arange(rows, dtype=jnp.int32)[None, :])
        .reshape(-1)
        .astype(jnp.float32)
    )
    q_width = heads_dev * HD
    tokens, mixed, docs = [], [], []
    for far in range(0, count, 2):
        group = [
            part for near in range(far, min(far + 2, count)) for part in (planes[near], mirrored[near])
        ]
        group = jnp.concatenate(group, axis=0)
        mixed.append(jnp.dot(group[:, :depth], qkv_full, preferred_element_type=jnp.float32))
        docs.append(group[:, depth])
    mixed = jnp.concatenate(mixed, axis=0)
    docs = jnp.concatenate(docs, axis=0)
    length = mixed.shape[0]
    queries = mixed[:, :q_width].reshape(length, heads_dev, HD)
    queries = rotate(rms_scale(queries, q_gain), position).astype(jnp.bfloat16)
    keys = rotate(rms_scale(mixed[:, None, q_width : q_width + HD], k_gain), position)
    keys = keys[:, 0].astype(jnp.bfloat16)
    values = mixed[:, q_width + HD :].astype(jnp.bfloat16)
    context = attend(queries, keys, values, position, docs)
    total = 0.0
    for far in reversed(range(count)):
        begin = 2 * far * rows
        partial = jnp.dot(
            context[begin : begin + 2 * rows], out_full, preferred_element_type=jnp.float32
        ).astype(jnp.bfloat16)
        other = y_link.send(partial[rows:], 1)
        pair = partial[:rows].astype(jnp.float32) + other.astype(jnp.float32)
        if far > 0:
            pair = z_link.send(pair.astype(jnp.bfloat16), 2 * far).astype(jnp.float32)
        total = total + pair
    return total


def router_gates(ffn_in, router_weight, routes):
    experts = router_weight.shape[1]
    logits = jnp.dot(ffn_in, router_weight, preferred_element_type=jnp.float32)
    probs = jax.nn.softmax(logits, axis=-1)
    chosen = routes[:, :, None] == jnp.arange(experts, dtype=jnp.int32)[None, None, :]
    return probs, chosen


def plane_chunks(count):
    rest = list(range(1, count))
    return [[0]] + [rest[i : i + 2] for i in range(0, len(rest), 2)]


def added(kept, received):
    return (kept.astype(jnp.float32) + received.astype(jnp.float32)).astype(jnp.bfloat16)


def experts_gathered(ffn_in, router_weight, routes, in_weights, out_weights, links):
    x_link, core_link, y_link, z_link = links
    n_seq = y_link.size
    rows, depth = ffn_in.shape
    experts = router_weight.shape[1]
    width = out_weights[0].shape[0]
    ids = [(lax.axis_index("exp") ^ m) * n_seq + lax.axis_index("seq") for m in range(2)]

    probs, chosen = router_gates(ffn_in, router_weight, routes)
    picked = jnp.where(jnp.any(chosen, axis=1), probs, 0.0)
    gates = picked / jnp.sum(picked, axis=-1, keepdims=True)
    gate_high = gates.astype(jnp.bfloat16)
    gate_low = (gates - gate_high.astype(jnp.float32)).astype(jnp.bfloat16)
    extra = jnp.concatenate([gate_high, gate_low], axis=1)
    extra = jnp.pad(extra, ((0, 0), (0, -extra.shape[1] % 128)))
    tagged = jnp.concatenate([ffn_in, extra], axis=1)

    half = rows // 2
    planes = [tagged] + [z_link.send(tagged, 2 * far) for far in range(1, n_seq // 2)]
    chunks = plane_chunks(n_seq // 2)
    gathered = []
    for chunk in chunks:
        a = jnp.concatenate([planes[far][:half] for far in chunk], axis=0)
        b = jnp.concatenate([planes[far][half:] for far in chunk], axis=0)
        a = jnp.concatenate([a, x_link.send(a, 2)], axis=0)
        b = jnp.concatenate([b, y_link.send(b, 1)], axis=0)
        gathered.append(
            jnp.concatenate([a, y_link.send(a, 1), b, x_link.send(b, 2)], axis=0)
        )
    partials = []
    for tokens in gathered:
        table = tokens[:, depth:].astype(jnp.float32)
        lanes = jnp.arange(table.shape[1], dtype=jnp.int32)[None, :]
        partial = 0.0
        for m in range(2):
            mine = (lanes == ids[m]) | (lanes == ids[m] + experts)
            gate = jnp.sum(jnp.where(mine, table, 0.0), axis=1, keepdims=True)
            both = jnp.dot(tokens[:, :depth], in_weights[m], preferred_element_type=jnp.float32)
            act = (jax.nn.silu(both[:, :width]) * both[:, width:] * gate).astype(jnp.bfloat16)
            partial = partial + jnp.dot(act, out_weights[m], preferred_element_type=jnp.float32)
        partials.append(partial.astype(jnp.bfloat16))
    total = 0.0
    for at in list(range(1, len(chunks))) + [0]:
        chunk, partial = chunks[at], partials[at]
        part = len(chunk) * half
        a = added(partial[: 2 * part], y_link.send(partial[2 * part : 4 * part], 1))
        b = added(partial[4 * part : 6 * part], x_link.send(partial[6 * part :], 2))
        a = added(a[:part], x_link.send(a[part:], 2))
        b = added(b[:part], y_link.send(b[part:], 1))
        for place, far in enumerate(chunk):
            span = slice(place * half, (place + 1) * half)
            block = jnp.concatenate([a[span], b[span]], axis=0)
            if far > 0:
                block = z_link.send(block, 2 * far)
            total = total + block.astype(jnp.float32)
    return total


def experts_exchanged(ffn_in, router_weight, routes, expert_in, expert_out):
    tok_count = ffn_in.shape[0]
    experts = router_weight.shape[1]
    capacity = 2 * tok_count * TOPK // experts
    probs, chosen = router_gates(ffn_in, router_weight, routes)
    picked = jnp.sum(jnp.where(chosen, probs[:, None, :], 0.0), axis=-1)
    gates = picked / jnp.sum(picked, axis=-1, keepdims=True)
    flat_hot = chosen.reshape(tok_count * TOPK, experts).astype(jnp.int32)
    before = jnp.cumsum(flat_hot, axis=0) - flat_hot
    slots = jnp.sum(before * flat_hot, axis=-1).reshape(tok_count, TOPK)
    slot_hot = slots[:, :, None] == jnp.arange(capacity, dtype=jnp.int32)[None, None, :]
    placing = jnp.sum(
        (chosen[:, :, :, None] & slot_hot[:, :, None, :]).astype(jnp.bfloat16), axis=1
    )
    sending = jnp.einsum("tec,td->ecd", placing, ffn_in, preferred_element_type=jnp.float32).astype(
        jnp.bfloat16
    )
    received = lax.all_to_all(sending, ("exp", "seq"), split_axis=0, concat_axis=0, tiled=True)
    flat = received.reshape(-1, received.shape[-1])
    both = jnp.dot(flat, expert_in[0], preferred_element_type=jnp.float32)
    width = expert_out.shape[1]
    act = (jax.nn.silu(both[:, :width]) * both[:, width:]).astype(jnp.bfloat16)
    result = jnp.dot(act, expert_out[0], preferred_element_type=jnp.float32).astype(jnp.bfloat16)
    returned = lax.all_to_all(
        result.reshape(received.shape), ("exp", "seq"), split_axis=0, concat_axis=0, tiled=True
    )
    index = (routes * capacity + slots).reshape(-1)
    rows = jnp.take(returned.reshape(experts * capacity, -1), index, axis=0).reshape(
        tok_count, TOPK, -1
    )
    mixture = jnp.einsum("tk,tkd->td", gates, rows.astype(jnp.float32))
    return mixture


def local(
    hidden_in,
    doc_ids,
    attn_gain,
    q_weight,
    kv_weight,
    q_gain,
    k_gain,
    out_weight,
    ffn_gain,
    router_weight,
    routes,
    expert_in,
    expert_out,
    *,
    n_exp,
    n_seq,
):
    links = (Link("exp", n_exp), Link("exp", n_exp), Link("seq", n_seq), Link("seq", n_seq, 2))
    attn_rows = attention_rows(
        hidden_in, doc_ids, attn_gain, q_weight, kv_weight, q_gain, k_gain, out_weight, links
    )
    tok_count = hidden_in.shape[0]
    capacity = 2 * tok_count * TOPK // router_weight.shape[1]
    gathering = n_exp == 4 and 2 * capacity >= tok_count
    if gathering:
        in_weights = [expert_in[0], links[1].send(expert_in[0], 1)]
        out_weights = [expert_out[0], links[1].send(expert_out[0], 1)]
    mid = (hidden_in.astype(jnp.float32) + attn_rows).astype(jnp.bfloat16)
    ffn_in = rms_scale(mid.astype(jnp.float32), ffn_gain).astype(jnp.bfloat16)
    if gathering:
        mixture = experts_gathered(ffn_in, router_weight, routes, in_weights, out_weights, links)
    else:
        mixture = experts_exchanged(ffn_in, router_weight, routes, expert_in, expert_out)
    return (mid.astype(jnp.float32) + mixture).astype(jnp.bfloat16)


def solution(mesh):
    in_specs = (
        P(("exp", "seq"), None),
        P(("exp", "seq")),
        P(),
        P("exp", "seq"),
        P(None, "exp", None),
        P(),
        P(),
        P("seq", "exp"),
        P(),
        P(),
        P(("exp", "seq"), None),
        P(("exp", "seq"), None, None),
        P(("exp", "seq"), None, None),
    )
    out_specs = P(("exp", "seq"), None)
    body = functools.partial(local, n_exp=mesh.shape["exp"], n_seq=mesh.shape["seq"])
    return jax.shard_map(body, mesh=mesh, in_specs=in_specs, out_specs=out_specs, check_vma=False)
```

```python
import functools
import math

import jax
import jax.numpy as jnp
from jax import lax
from jax.sharding import PartitionSpec as P

HEADS = 32
KV = 4
HD = 128
TOPK = 8


def rms_scale(values, gain):
    return values * lax.rsqrt(jnp.mean(values * values, axis=-1, keepdims=True) + 1e-06) * gain


def rotate(values, position):
    half = values.shape[-1] // 2
    freq = jnp.exp(
        -(2.0 * jnp.arange(half, dtype=jnp.float32) / values.shape[-1]) * math.log(1000000.0)
    )
    angle = position[:, None, None] * freq
    cosine = jnp.cos(angle)
    sine = jnp.sin(angle)
    first = values[..., :half]
    second = values[..., half:]
    return jnp.concatenate(
        [first * cosine - second * sine, second * cosine + first * sine], axis=-1
    )


class Link:
    def __init__(self, axis, size, depth=1):
        self.axis, self.size, self.depth = axis, size, depth
        self.results = []

    def send(self, values, mask, after=()):
        waits = self.results[-self.depth :][:1] if len(self.results) >= self.depth else []
        waits = tuple(waits) + tuple(after)
        if waits:
            values = lax.optimization_barrier((values, waits))[0]
        result = lax.ppermute(values, self.axis, [(i, i ^ mask) for i in range(self.size)])
        self.results.append(result)
        return result


def attend(queries, keys, values, position, docs):
    scale = 1.0 / math.sqrt(keys.shape[-1])
    scores = jnp.einsum("qhd,kd->hqk", queries, keys, preferred_element_type=jnp.float32) * scale
    allowed = (position[None, :] <= position[:, None]) & (docs[None, :] == docs[:, None])
    scores = jnp.where(allowed[None], scores, -1e30)
    top = jnp.max(scores, axis=-1, keepdims=True)
    expo = jnp.exp(scores - top)
    weights = (expo / jnp.sum(expo, axis=-1, keepdims=True)).astype(jnp.bfloat16)
    context = jnp.einsum(
        "hqk,kd->qhd", weights, values, preferred_element_type=jnp.float32
    ).astype(jnp.bfloat16)
    return context.reshape(queries.shape[0], -1)


def plane_order(count):
    return [0, 1, 3, 2] if count == 4 else list(range(count))


def attention_rows(
    hidden_in, doc_ids, attn_gain, q_weight, kv_weight, q_gain, k_gain, out_weight, links
):
    x_link, core_link, y_link, z_link = links
    n_exp, n_seq = x_link.size, y_link.size
    own_exp = lax.axis_index("exp")
    own_seq = lax.axis_index("seq")
    heads_dev = q_weight.shape[1] // HD
    rows, depth = hidden_in.shape
    count = n_seq // 2
    normed = rms_scale(hidden_in.astype(jnp.float32), attn_gain).astype(jnp.bfloat16)
    tagged = jnp.concatenate(
        [normed, jnp.broadcast_to(doc_ids.astype(jnp.bfloat16)[:, None], (rows, 128))], axis=1
    )
    fars = plane_order(count)
    planes = [tagged]
    mirrored = [y_link.send(tagged, 1)]
    for far in fars[1:]:
        planes.append(z_link.send(tagged, 2 * far))
    kv_local = lax.dynamic_index_in_dim(
        kv_weight, own_seq * heads_dev // (HEADS // KV), 0, keepdims=False
    )
    qkv_shard = jnp.concatenate([q_weight, kv_local], axis=1)
    qkv_pieces, out_pieces = [], []
    for shard, pieces in ((qkv_shard, qkv_pieces), (out_weight, out_pieces)):
        for far in range(n_exp // 2):
            near = shard if far == 0 else x_link.send(shard, 2 * far)
            pieces += [near, core_link.send(near, 1)]
    for far in range(1, count):
        mirrored.append(y_link.send(planes[far], 1))
    span = q_weight.shape[0]
    qkv_full = jnp.zeros((depth, qkv_shard.shape[1]), jnp.bfloat16)
    out_full = jnp.zeros((out_weight.shape[0], depth), jnp.bfloat16)
    for m in range(n_exp):
        start = (own_exp ^ m) * span
        qkv_full = lax.dynamic_update_slice(qkv_full, qkv_pieces[m], (start, 0))
        out_full = lax.dynamic_update_slice(out_full, out_pieces[m], (0, start))

    order = own_seq ^ jnp.array([2 * far + side for far in fars for side in range(2)], jnp.int32)
    position = (
        (order[:, None] * rows + jnp.arange(rows, dtype=jnp.int32)[None, :])
        .reshape(-1)
        .astype(jnp.float32)
    )
    q_width = heads_dev * HD
    tokens, mixed, docs = [], [], []
    for far in range(0, count, 2):
        group = [
            part for near in range(far, min(far + 2, count)) for part in (planes[near], mirrored[near])
        ]
        group = jnp.concatenate(group, axis=0)
        mixed.append(jnp.dot(group[:, :depth], qkv_full, preferred_element_type=jnp.float32))
        docs.append(group[:, depth])
    mixed = jnp.concatenate(mixed, axis=0)
    docs = jnp.concatenate(docs, axis=0)
    length = mixed.shape[0]
    queries = mixed[:, :q_width].reshape(length, heads_dev, HD)
    queries = rotate(rms_scale(queries, q_gain), position).astype(jnp.bfloat16)
    keys = rotate(rms_scale(mixed[:, None, q_width : q_width + HD], k_gain), position)
    keys = keys[:, 0].astype(jnp.bfloat16)
    values = mixed[:, q_width + HD :].astype(jnp.bfloat16)
    context = attend(queries, keys, values, position, docs)
    total = 0.0
    for place in reversed(range(count)):
        far = fars[place]
        begin = 2 * place * rows
        partial = jnp.dot(
            context[begin : begin + 2 * rows], out_full, preferred_element_type=jnp.float32
        ).astype(jnp.bfloat16)
        other = y_link.send(partial[rows:], 1)
        pair = partial[:rows].astype(jnp.float32) + other.astype(jnp.float32)
        if far > 0:
            pair = z_link.send(pair.astype(jnp.bfloat16), 2 * far).astype(jnp.float32)
        total = total + pair
    return total


def router_gates(ffn_in, router_weight, routes):
    experts = router_weight.shape[1]
    logits = jnp.dot(ffn_in, router_weight, preferred_element_type=jnp.float32)
    probs = jax.nn.softmax(logits, axis=-1)
    chosen = routes[:, :, None] == jnp.arange(experts, dtype=jnp.int32)[None, None, :]
    return probs, chosen


def added(kept, received):
    return (kept.astype(jnp.float32) + received.astype(jnp.float32)).astype(jnp.bfloat16)


def experts_gathered(ffn_in, router_weight, routes, in_weights, out_weights, links):
    x_link, core_link, y_link, z_link = links
    x_link.depth = y_link.depth = 2
    n_seq = y_link.size
    rows, depth = ffn_in.shape
    experts = router_weight.shape[1]
    width = out_weights[0].shape[0]
    ids = [(lax.axis_index("exp") ^ m) * n_seq + lax.axis_index("seq") for m in range(2)]

    probs, chosen = router_gates(ffn_in, router_weight, routes)
    picked = jnp.where(jnp.any(chosen, axis=1), probs, 0.0)
    gates = picked / jnp.sum(picked, axis=-1, keepdims=True)
    gate_high = gates.astype(jnp.bfloat16)
    gate_low = (gates - gate_high.astype(jnp.float32)).astype(jnp.bfloat16)
    extra = jnp.concatenate([gate_high, gate_low], axis=1)
    extra = jnp.pad(extra, ((0, 0), (0, -extra.shape[1] % 128)))
    tagged = jnp.concatenate([ffn_in, extra], axis=1)

    half = rows // 2
    planes = {0: tagged, 1: z_link.send(tagged, 2), 3: z_link.send(tagged, 6)}
    planes[2] = jnp.concatenate(
        [z_link.send(planes[1][:half], 6), z_link.send(planes[3][half:], 2)], axis=0
    )
    chunks = [[0], [1, 3], [2]]
    gathered = []
    for chunk in chunks:
        a = jnp.concatenate([planes[far][:half] for far in chunk], axis=0)
        b = jnp.concatenate([planes[far][half:] for far in chunk], axis=0)
        a = jnp.concatenate([a, x_link.send(a, 2)], axis=0)
        b = jnp.concatenate([b, y_link.send(b, 1)], axis=0)
        gathered.append(
            jnp.concatenate([a, y_link.send(a, 1), b, x_link.send(b, 2)], axis=0)
        )
    partials = []
    for tokens in gathered:
        if partials:
            tokens = lax.optimization_barrier((tokens, partials[-1]))[0]
        table = tokens[:, depth:].astype(jnp.float32)
        lanes = jnp.arange(table.shape[1], dtype=jnp.int32)[None, :]
        partial = 0.0
        for m in range(2):
            mine = (lanes == ids[m]) | (lanes == ids[m] + experts)
            gate = jnp.sum(jnp.where(mine, table, 0.0), axis=1, keepdims=True)
            both = jnp.dot(tokens[:, :depth], in_weights[m], preferred_element_type=jnp.float32)
            act = (jax.nn.silu(both[:, :width]) * both[:, width:] * gate).astype(jnp.bfloat16)
            partial = partial + jnp.dot(act, out_weights[m], preferred_element_type=jnp.float32)
        partials.append(partial.astype(jnp.bfloat16))
    total = 0.0
    for chunk, partial in zip(chunks, partials):
        part = len(chunk) * half
        a = added(partial[: 2 * part], y_link.send(partial[2 * part : 4 * part], 1))
        b = added(partial[4 * part : 6 * part], x_link.send(partial[6 * part :], 2))
        a = added(a[:part], x_link.send(a[part:], 2))
        b = added(b[:part], y_link.send(b[part:], 1))
        for place, far in enumerate(chunk):
            span = slice(place * half, (place + 1) * half)
            if far == 2:
                through = [z_link.send(a[span], 2), z_link.send(b[span], 6)]
                block = [z_link.send(through[0], 6), z_link.send(through[1], 2)]
                block = jnp.concatenate(block, axis=0)
            else:
                block = jnp.concatenate([a[span], b[span]], axis=0)
                if far > 0:
                    block = z_link.send(block, 2 * far)
            total = total + block.astype(jnp.float32)
    return total


def experts_exchanged(ffn_in, router_weight, routes, expert_in, expert_out):
    tok_count = ffn_in.shape[0]
    experts = router_weight.shape[1]
    capacity = 2 * tok_count * TOPK // experts
    probs, chosen = router_gates(ffn_in, router_weight, routes)
    picked = jnp.sum(jnp.where(chosen, probs[:, None, :], 0.0), axis=-1)
    gates = picked / jnp.sum(picked, axis=-1, keepdims=True)
    flat_hot = chosen.reshape(tok_count * TOPK, experts).astype(jnp.int32)
    before = jnp.cumsum(flat_hot, axis=0) - flat_hot
    slots = jnp.sum(before * flat_hot, axis=-1).reshape(tok_count, TOPK)
    slot_hot = slots[:, :, None] == jnp.arange(capacity, dtype=jnp.int32)[None, None, :]
    placing = jnp.sum(
        (chosen[:, :, :, None] & slot_hot[:, :, None, :]).astype(jnp.bfloat16), axis=1
    )
    sending = jnp.einsum("tec,td->ecd", placing, ffn_in, preferred_element_type=jnp.float32).astype(
        jnp.bfloat16
    )
    received = lax.all_to_all(sending, ("exp", "seq"), split_axis=0, concat_axis=0, tiled=True)
    flat = received.reshape(-1, received.shape[-1])
    both = jnp.dot(flat, expert_in[0], preferred_element_type=jnp.float32)
    width = expert_out.shape[1]
    act = (jax.nn.silu(both[:, :width]) * both[:, width:]).astype(jnp.bfloat16)
    result = jnp.dot(act, expert_out[0], preferred_element_type=jnp.float32).astype(jnp.bfloat16)
    returned = lax.all_to_all(
        result.reshape(received.shape), ("exp", "seq"), split_axis=0, concat_axis=0, tiled=True
    )
    index = (routes * capacity + slots).reshape(-1)
    rows = jnp.take(returned.reshape(experts * capacity, -1), index, axis=0).reshape(
        tok_count, TOPK, -1
    )
    mixture = jnp.einsum("tk,tkd->td", gates, rows.astype(jnp.float32))
    return mixture


def local(
    hidden_in,
    doc_ids,
    attn_gain,
    q_weight,
    kv_weight,
    q_gain,
    k_gain,
    out_weight,
    ffn_gain,
    router_weight,
    routes,
    expert_in,
    expert_out,
    *,
    n_exp,
    n_seq,
):
    links = (Link("exp", n_exp), Link("exp", n_exp), Link("seq", n_seq), Link("seq", n_seq, 2))
    attn_rows = attention_rows(
        hidden_in, doc_ids, attn_gain, q_weight, kv_weight, q_gain, k_gain, out_weight, links
    )
    tok_count = hidden_in.shape[0]
    capacity = 2 * tok_count * TOPK // router_weight.shape[1]
    gathering = n_exp == 4 and n_seq == 8 and 2 * capacity >= tok_count
    if gathering:
        in_weights = [expert_in[0], links[1].send(expert_in[0], 1)]
        out_weights = [expert_out[0], links[1].send(expert_out[0], 1)]
    mid = (hidden_in.astype(jnp.float32) + attn_rows).astype(jnp.bfloat16)
    ffn_in = rms_scale(mid.astype(jnp.float32), ffn_gain).astype(jnp.bfloat16)
    if gathering:
        mixture = experts_gathered(ffn_in, router_weight, routes, in_weights, out_weights, links)
    else:
        mixture = experts_exchanged(ffn_in, router_weight, routes, expert_in, expert_out)
    return (mid.astype(jnp.float32) + mixture).astype(jnp.bfloat16)


def solution(mesh):
    in_specs = (
        P(("exp", "seq"), None),
        P(("exp", "seq")),
        P(),
        P("exp", "seq"),
        P(None, "exp", None),
        P(),
        P(),
        P("seq", "exp"),
        P(),
        P(),
        P(("exp", "seq"), None),
        P(("exp", "seq"), None, None),
        P(("exp", "seq"), None, None),
    )
    out_specs = P(("exp", "seq"), None)
    body = functools.partial(local, n_exp=mesh.shape["exp"], n_seq=mesh.shape["seq"])
    return jax.shard_map(body, mesh=mesh, in_specs=in_specs, out_specs=out_specs, check_vma=False)
```

```python
import functools
import math

import jax
import jax.numpy as jnp
from jax import lax
from jax.sharding import PartitionSpec as P

HEADS = 32
KV = 4
HD = 128
TOPK = 8


def rms_scale(values, gain):
    return values * lax.rsqrt(jnp.mean(values * values, axis=-1, keepdims=True) + 1e-06) * gain


def rotate(values, position):
    half = values.shape[-1] // 2
    freq = jnp.exp(
        -(2.0 * jnp.arange(half, dtype=jnp.float32) / values.shape[-1]) * math.log(1000000.0)
    )
    angle = position[:, None, None] * freq
    cosine = jnp.cos(angle)
    sine = jnp.sin(angle)
    first = values[..., :half]
    second = values[..., half:]
    return jnp.concatenate(
        [first * cosine - second * sine, second * cosine + first * sine], axis=-1
    )


class Link:
    def __init__(self, axis, size, depth=1):
        self.axis, self.size, self.depth = axis, size, depth
        self.results = []

    def send(self, values, mask, after=()):
        waits = self.results[-self.depth :][:1] if len(self.results) >= self.depth else []
        waits = tuple(waits) + tuple(after)
        if waits:
            values = lax.optimization_barrier((values, waits))[0]
        result = lax.ppermute(values, self.axis, [(i, i ^ mask) for i in range(self.size)])
        self.results.append(result)
        return result


def attend(queries, keys, values, position, docs):
    scale = 1.0 / math.sqrt(keys.shape[-1])
    scores = jnp.einsum("qhd,kd->hqk", queries, keys, preferred_element_type=jnp.float32) * scale
    allowed = (position[None, :] <= position[:, None]) & (docs[None, :] == docs[:, None])
    scores = jnp.where(allowed[None], scores, -1e30)
    top = jnp.max(scores, axis=-1, keepdims=True)
    expo = jnp.exp(scores - top)
    weights = (expo / jnp.sum(expo, axis=-1, keepdims=True)).astype(jnp.bfloat16)
    context = jnp.einsum(
        "hqk,kd->qhd", weights, values, preferred_element_type=jnp.float32
    ).astype(jnp.bfloat16)
    return context.reshape(queries.shape[0], -1)


def attention_rows(
    hidden_in, doc_ids, attn_gain, q_weight, kv_weight, q_gain, k_gain, out_weight, links, swapping
):
    x_link, core_link, y_link, z_link = links
    n_exp, n_seq = x_link.size, y_link.size
    own_exp = lax.axis_index("exp")
    own_seq = lax.axis_index("seq")
    heads_dev = q_weight.shape[1] // HD
    rows, depth = hidden_in.shape
    count = n_seq // 2
    normed = rms_scale(hidden_in.astype(jnp.float32), attn_gain).astype(jnp.bfloat16)
    tagged = jnp.concatenate(
        [normed, jnp.broadcast_to(doc_ids.astype(jnp.bfloat16)[:, None], (rows, 128))], axis=1
    )
    planes = [tagged]
    mirrored = [y_link.send(tagged, 1)]
    for far in range(1, count):
        planes.append(z_link.send(tagged, 2 * far))
    kv_local = lax.dynamic_index_in_dim(
        kv_weight, own_seq * heads_dev // (HEADS // KV), 0, keepdims=False
    )
    qkv_shard = jnp.concatenate([q_weight, kv_local], axis=1)
    qkv_pieces, out_pieces = [], []
    for shard, pieces in ((qkv_shard, qkv_pieces), (out_weight, out_pieces)):
        for far in range(n_exp // 2):
            near = shard if far == 0 else x_link.send(shard, 2 * far)
            pieces += [near, core_link.send(near, 1)]
    for far in range(1, count):
        mirrored.append(y_link.send(planes[far], 1))
    swapped = []
    for weight in swapping:
        after = tuple(planes[2:3]) + tuple(swapped)
        swapped.append(Link("exp", n_exp).send(weight, 1, after))
    span = q_weight.shape[0]
    qkv_full = jnp.zeros((depth, qkv_shard.shape[1]), jnp.bfloat16)
    out_full = jnp.zeros((out_weight.shape[0], depth), jnp.bfloat16)
    for m in range(n_exp):
        start = (own_exp ^ m) * span
        qkv_full = lax.dynamic_update_slice(qkv_full, qkv_pieces[m], (start, 0))
        out_full = lax.dynamic_update_slice(out_full, out_pieces[m], (0, start))

    order = own_seq ^ jnp.arange(n_seq, dtype=jnp.int32)
    position = (
        (order[:, None] * rows + jnp.arange(rows, dtype=jnp.int32)[None, :])
        .reshape(-1)
        .astype(jnp.float32)
    )
    q_width = heads_dev * HD
    tokens, mixed, docs = [], [], []
    for far in range(0, count, 2):
        group = [
            part for near in range(far, min(far + 2, count)) for part in (planes[near], mirrored[near])
        ]
        group = jnp.concatenate(group, axis=0)
        mixed.append(jnp.dot(group[:, :depth], qkv_full, preferred_element_type=jnp.float32))
        docs.append(group[:, depth])
    mixed = jnp.concatenate(mixed, axis=0)
    docs = jnp.concatenate(docs, axis=0)
    length = mixed.shape[0]
    queries = mixed[:, :q_width].reshape(length, heads_dev, HD)
    queries = rotate(rms_scale(queries, q_gain), position).astype(jnp.bfloat16)
    keys = rotate(rms_scale(mixed[:, None, q_width : q_width + HD], k_gain), position)
    keys = keys[:, 0].astype(jnp.bfloat16)
    values = mixed[:, q_width + HD :].astype(jnp.bfloat16)
    context = attend(queries, keys, values, position, docs)
    total = 0.0
    if swapped:
        context, swapped[0] = lax.optimization_barrier((context, swapped[0]))
    for far in reversed(range(count)):
        begin = 2 * far * rows
        partial = jnp.dot(
            context[begin : begin + 2 * rows], out_full, preferred_element_type=jnp.float32
        ).astype(jnp.bfloat16)
        other = y_link.send(partial[rows:], 1, swapped if far == 0 else ())
        pair = partial[:rows].astype(jnp.float32) + other.astype(jnp.float32)
        if far > 0:
            pair = z_link.send(pair.astype(jnp.bfloat16), 2 * far).astype(jnp.float32)
        total = total + pair
    return total, swapped


def router_gates(ffn_in, router_weight, routes):
    experts = router_weight.shape[1]
    logits = jnp.dot(ffn_in, router_weight, preferred_element_type=jnp.float32)
    probs = jax.nn.softmax(logits, axis=-1)
    chosen = routes[:, :, None] == jnp.arange(experts, dtype=jnp.int32)[None, None, :]
    return probs, chosen


def plane_chunks(count):
    rest = list(range(1, count))
    return [[0]] + [rest[i : i + 2] for i in range(0, len(rest), 2)]


def added(kept, received):
    return (kept.astype(jnp.float32) + received.astype(jnp.float32)).astype(jnp.bfloat16)


def experts_gathered(ffn_in, router_weight, routes, in_weights, out_weights, links):
    x_link, core_link, y_link, z_link = links
    n_seq = y_link.size
    rows, depth = ffn_in.shape
    experts = router_weight.shape[1]
    width = out_weights[0].shape[0]
    ids = [(lax.axis_index("exp") ^ m) * n_seq + lax.axis_index("seq") for m in range(2)]

    probs, chosen = router_gates(ffn_in, router_weight, routes)
    picked = jnp.where(jnp.any(chosen, axis=1), probs, 0.0)
    gates = picked / jnp.sum(picked, axis=-1, keepdims=True)
    gate_high = gates.astype(jnp.bfloat16)
    gate_low = (gates - gate_high.astype(jnp.float32)).astype(jnp.bfloat16)
    extra = jnp.concatenate([gate_high, gate_low], axis=1)
    extra = jnp.pad(extra, ((0, 0), (0, -extra.shape[1] % 128)))
    tagged = jnp.concatenate([ffn_in, extra], axis=1)

    half = rows // 2
    planes = [tagged] + [z_link.send(tagged, 2 * far) for far in range(1, n_seq // 2)]
    chunks = plane_chunks(n_seq // 2)

    def first_step(chunk, after=()):
        a = jnp.concatenate([planes[far][:half] for far in chunk], axis=0)
        b = jnp.concatenate([planes[far][half:] for far in chunk], axis=0)
        a = jnp.concatenate([a, x_link.send(a, 2, after)], axis=0)
        b = jnp.concatenate([b, y_link.send(b, 1, after)], axis=0)
        return a, b

    def second_step(a, b, after=()):
        return jnp.concatenate([a, y_link.send(a, 1, after), b, x_link.send(b, 2, after)], axis=0)

    def activations(tokens):
        table = tokens[:, depth:].astype(jnp.float32)
        lanes = jnp.arange(table.shape[1], dtype=jnp.int32)[None, :]
        acts = []
        for m in range(2):
            mine = (lanes == ids[m]) | (lanes == ids[m] + experts)
            gate = jnp.sum(jnp.where(mine, table, 0.0), axis=1, keepdims=True)
            both = jnp.dot(tokens[:, :depth], in_weights[m], preferred_element_type=jnp.float32)
            acts.append((jax.nn.silu(both[:, :width]) * both[:, width:] * gate).astype(jnp.bfloat16))
        return acts

    def results(acts):
        partial = 0.0
        for act, weight in zip(acts, out_weights):
            partial = partial + jnp.dot(act, weight, preferred_element_type=jnp.float32)
        return partial.astype(jnp.bfloat16)

    def first_return(partial, after=()):
        part = partial.shape[0] // 8
        a = added(partial[: 2 * part], y_link.send(partial[2 * part : 4 * part], 1, after))
        b = added(partial[4 * part : 6 * part], x_link.send(partial[6 * part :], 2, after))
        return a, b

    def second_return(a, b, after=()):
        part = a.shape[0] // 2
        a = added(a[:part], x_link.send(a[part:], 2, after))
        b = added(b[:part], y_link.send(b[part:], 1, after))
        return a, b

    def home(chunk, a, b):
        total = 0.0
        for place, far in enumerate(chunk):
            span = slice(place * half, (place + 1) * half)
            block = jnp.concatenate([a[span], b[span]], axis=0)
            if far > 0:
                block = z_link.send(block, 2 * far)
            total = total + block.astype(jnp.float32)
        return total

    tokens0 = second_step(*first_step(chunks[0]))
    ahead1 = first_step(chunks[1])
    acts0 = activations(tokens0)
    tokens1 = second_step(*ahead1, acts0)
    partial0 = results(acts0)
    ahead2 = first_step(chunks[2], (partial0,))
    back0 = first_return(partial0)
    acts1 = activations(tokens1)
    tokens2 = second_step(*ahead2, acts1[:1])
    back0 = second_return(*back0, acts1[:1])
    partial1 = results(acts1)
    back1 = first_return(partial1)
    tokens2 = lax.optimization_barrier((tokens2, partial1))[0]
    acts2 = activations(tokens2)
    back1 = second_return(*back1, acts2)
    partial2 = results(acts2)
    total = home(chunks[1], *back1)
    back2 = second_return(*first_return(partial2))
    return total + home(chunks[0], *back0) + home(chunks[2], *back2)


def experts_exchanged(ffn_in, router_weight, routes, expert_in, expert_out):
    tok_count = ffn_in.shape[0]
    experts = router_weight.shape[1]
    capacity = 2 * tok_count * TOPK // experts
    probs, chosen = router_gates(ffn_in, router_weight, routes)
    picked = jnp.sum(jnp.where(chosen, probs[:, None, :], 0.0), axis=-1)
    gates = picked / jnp.sum(picked, axis=-1, keepdims=True)
    flat_hot = chosen.reshape(tok_count * TOPK, experts).astype(jnp.int32)
    before = jnp.cumsum(flat_hot, axis=0) - flat_hot
    slots = jnp.sum(before * flat_hot, axis=-1).reshape(tok_count, TOPK)
    slot_hot = slots[:, :, None] == jnp.arange(capacity, dtype=jnp.int32)[None, None, :]
    placing = jnp.sum(
        (chosen[:, :, :, None] & slot_hot[:, :, None, :]).astype(jnp.bfloat16), axis=1
    )
    sending = jnp.einsum("tec,td->ecd", placing, ffn_in, preferred_element_type=jnp.float32).astype(
        jnp.bfloat16
    )
    received = lax.all_to_all(sending, ("exp", "seq"), split_axis=0, concat_axis=0, tiled=True)
    flat = received.reshape(-1, received.shape[-1])
    both = jnp.dot(flat, expert_in[0], preferred_element_type=jnp.float32)
    width = expert_out.shape[1]
    act = (jax.nn.silu(both[:, :width]) * both[:, width:]).astype(jnp.bfloat16)
    result = jnp.dot(act, expert_out[0], preferred_element_type=jnp.float32).astype(jnp.bfloat16)
    returned = lax.all_to_all(
        result.reshape(received.shape), ("exp", "seq"), split_axis=0, concat_axis=0, tiled=True
    )
    index = (routes * capacity + slots).reshape(-1)
    rows = jnp.take(returned.reshape(experts * capacity, -1), index, axis=0).reshape(
        tok_count, TOPK, -1
    )
    mixture = jnp.einsum("tk,tkd->td", gates, rows.astype(jnp.float32))
    return mixture


def local(
    hidden_in,
    doc_ids,
    attn_gain,
    q_weight,
    kv_weight,
    q_gain,
    k_gain,
    out_weight,
    ffn_gain,
    router_weight,
    routes,
    expert_in,
    expert_out,
    *,
    n_exp,
    n_seq,
):
    links = (Link("exp", n_exp), Link("exp", n_exp), Link("seq", n_seq), Link("seq", n_seq, 2))
    tok_count = hidden_in.shape[0]
    capacity = 2 * tok_count * TOPK // router_weight.shape[1]
    gathering = n_exp == 4 and n_seq == 8 and 2 * capacity >= tok_count
    attn_rows, swapped = attention_rows(
        hidden_in,
        doc_ids,
        attn_gain,
        q_weight,
        kv_weight,
        q_gain,
        k_gain,
        out_weight,
        links,
        (expert_in[0], expert_out[0]) if gathering else (),
    )
    mid = (hidden_in.astype(jnp.float32) + attn_rows).astype(jnp.bfloat16)
    ffn_in = rms_scale(mid.astype(jnp.float32), ffn_gain).astype(jnp.bfloat16)
    if gathering:
        in_weights, out_weights = [expert_in[0], swapped[0]], [expert_out[0], swapped[1]]
        mixture = experts_gathered(ffn_in, router_weight, routes, in_weights, out_weights, links)
    else:
        mixture = experts_exchanged(ffn_in, router_weight, routes, expert_in, expert_out)
    return (mid.astype(jnp.float32) + mixture).astype(jnp.bfloat16)


def solution(mesh):
    in_specs = (
        P(("exp", "seq"), None),
        P(("exp", "seq")),
        P(),
        P("exp", "seq"),
        P(None, "exp", None),
        P(),
        P(),
        P("seq", "exp"),
        P(),
        P(),
        P(("exp", "seq"), None),
        P(("exp", "seq"), None, None),
        P(("exp", "seq"), None, None),
    )
    out_specs = P(("exp", "seq"), None)
    body = functools.partial(local, n_exp=mesh.shape["exp"], n_seq=mesh.shape["seq"])
    return jax.shard_map(body, mesh=mesh, in_specs=in_specs, out_specs=out_specs, check_vma=False)
```

```python
import functools
import math

import jax
import jax.numpy as jnp
from jax import lax
from jax.sharding import PartitionSpec as P

HEADS = 32
KV = 4
HD = 128
TOPK = 8


def rms_scale(values, gain):
    return values * lax.rsqrt(jnp.mean(values * values, axis=-1, keepdims=True) + 1e-06) * gain


def rotate(values, position):
    half = values.shape[-1] // 2
    freq = jnp.exp(
        -(2.0 * jnp.arange(half, dtype=jnp.float32) / values.shape[-1]) * math.log(1000000.0)
    )
    angle = position[:, None, None] * freq
    cosine = jnp.cos(angle)
    sine = jnp.sin(angle)
    first = values[..., :half]
    second = values[..., half:]
    return jnp.concatenate(
        [first * cosine - second * sine, second * cosine + first * sine], axis=-1
    )


class Link:
    def __init__(self, axis, size, depth=1):
        self.axis, self.size, self.depth = axis, size, depth
        self.results = []

    def send(self, values, mask, after=()):
        waits = self.results[-self.depth :][:1] if len(self.results) >= self.depth else []
        waits = tuple(waits) + tuple(after)
        if waits:
            values = lax.optimization_barrier((values, waits))[0]
        result = lax.ppermute(values, self.axis, [(i, i ^ mask) for i in range(self.size)])
        self.results.append(result)
        return result


def attend(queries, keys, values, position, docs):
    scale = 1.0 / math.sqrt(keys.shape[-1])
    scores = jnp.einsum("qhd,kd->hqk", queries, keys, preferred_element_type=jnp.float32) * scale
    allowed = (position[None, :] <= position[:, None]) & (docs[None, :] == docs[:, None])
    scores = jnp.where(allowed[None], scores, -1e30)
    top = jnp.max(scores, axis=-1, keepdims=True)
    expo = jnp.exp(scores - top)
    weights = (expo / jnp.sum(expo, axis=-1, keepdims=True)).astype(jnp.bfloat16)
    context = jnp.einsum(
        "hqk,kd->qhd", weights, values, preferred_element_type=jnp.float32
    ).astype(jnp.bfloat16)
    return context.reshape(queries.shape[0], -1)


def attention_rows(
    hidden_in, doc_ids, attn_gain, q_weight, kv_weight, q_gain, k_gain, out_weight, links
):
    x_link, core_link, y_link, z_link = links
    n_exp, n_seq = x_link.size, y_link.size
    own_exp = lax.axis_index("exp")
    own_seq = lax.axis_index("seq")
    heads_dev = q_weight.shape[1] // HD
    rows, depth = hidden_in.shape
    count = n_seq // 2
    normed = rms_scale(hidden_in.astype(jnp.float32), attn_gain).astype(jnp.bfloat16)
    tagged = jnp.concatenate(
        [normed, jnp.broadcast_to(doc_ids.astype(jnp.bfloat16)[:, None], (rows, 128))], axis=1
    )
    planes = [tagged]
    mirrored = [y_link.send(tagged, 1)]
    for far in range(1, count):
        planes.append(z_link.send(tagged, 2 * far))
    kv_local = lax.dynamic_index_in_dim(
        kv_weight, own_seq * heads_dev // (HEADS // KV), 0, keepdims=False
    )
    qkv_shard = jnp.concatenate([q_weight, kv_local], axis=1)
    qkv_pieces, out_pieces = [], []
    for shard, pieces in ((qkv_shard, qkv_pieces), (out_weight, out_pieces)):
        for far in range(n_exp // 2):
            near = shard if far == 0 else x_link.send(shard, 2 * far)
            pieces += [near, core_link.send(near, 1)]
    for far in range(1, count):
        mirrored.append(y_link.send(planes[far], 1))
    span = q_weight.shape[0]
    qkv_full = jnp.zeros((depth, qkv_shard.shape[1]), jnp.bfloat16)
    out_full = jnp.zeros((out_weight.shape[0], depth), jnp.bfloat16)
    for m in range(n_exp):
        start = (own_exp ^ m) * span
        qkv_full = lax.dynamic_update_slice(qkv_full, qkv_pieces[m], (start, 0))
        out_full = lax.dynamic_update_slice(out_full, out_pieces[m], (0, start))

    order = own_seq ^ jnp.arange(n_seq, dtype=jnp.int32)
    position = (
        (order[:, None] * rows + jnp.arange(rows, dtype=jnp.int32)[None, :])
        .reshape(-1)
        .astype(jnp.float32)
    )
    q_width = heads_dev * HD
    tokens, mixed, docs = [], [], []
    for far in range(0, count, 2):
        group = [
            part for near in range(far, min(far + 2, count)) for part in (planes[near], mirrored[near])
        ]
        group = jnp.concatenate(group, axis=0)
        mixed.append(jnp.dot(group[:, :depth], qkv_full, preferred_element_type=jnp.float32))
        docs.append(group[:, depth])
    mixed = jnp.concatenate(mixed, axis=0)
    docs = jnp.concatenate(docs, axis=0)
    length = mixed.shape[0]
    queries = mixed[:, :q_width].reshape(length, heads_dev, HD)
    queries = rotate(rms_scale(queries, q_gain), position).astype(jnp.bfloat16)
    keys = rotate(rms_scale(mixed[:, None, q_width : q_width + HD], k_gain), position)
    keys = keys[:, 0].astype(jnp.bfloat16)
    values = mixed[:, q_width + HD :].astype(jnp.bfloat16)
    context = attend(queries, keys, values, position, docs)
    total = 0.0
    for far in (*range(2, count), 1, 0):
        begin = 2 * far * rows
        partial = jnp.dot(
            context[begin : begin + 2 * rows], out_full, preferred_element_type=jnp.float32
        ).astype(jnp.bfloat16)
        other = y_link.send(partial[rows:], 1)
        pair = partial[:rows].astype(jnp.float32) + other.astype(jnp.float32)
        if far > 0:
            pair = z_link.send(pair.astype(jnp.bfloat16), 2 * far).astype(jnp.float32)
        total = total + pair
    return total


def router_gates(ffn_in, router_weight, routes):
    experts = router_weight.shape[1]
    logits = jnp.dot(ffn_in, router_weight, preferred_element_type=jnp.float32)
    probs = jax.nn.softmax(logits, axis=-1)
    chosen = routes[:, :, None] == jnp.arange(experts, dtype=jnp.int32)[None, None, :]
    return probs, chosen


def plane_chunks(count):
    rest = list(range(1, count))
    return [[0]] + [rest[i : i + 2] for i in range(0, len(rest), 2)]


def added(kept, received):
    return (kept.astype(jnp.float32) + received.astype(jnp.float32)).astype(jnp.bfloat16)


def experts_gathered(ffn_in, router_weight, routes, in_weights, out_weights, links):
    x_link, core_link, y_link, z_link = links
    n_seq = y_link.size
    rows, depth = ffn_in.shape
    experts = router_weight.shape[1]
    width = out_weights[0].shape[0]
    ids = [(lax.axis_index("exp") ^ m) * n_seq + lax.axis_index("seq") for m in range(2)]

    probs, chosen = router_gates(ffn_in, router_weight, routes)
    picked = jnp.where(jnp.any(chosen, axis=1), probs, 0.0)
    gates = picked / jnp.sum(picked, axis=-1, keepdims=True)
    gate_high = gates.astype(jnp.bfloat16)
    gate_low = (gates - gate_high.astype(jnp.float32)).astype(jnp.bfloat16)
    extra = jnp.concatenate([gate_high, gate_low], axis=1)
    extra = jnp.pad(extra, ((0, 0), (0, -extra.shape[1] % 128)))
    tagged = jnp.concatenate([ffn_in, extra], axis=1)

    half = rows // 2
    planes = [tagged] + [z_link.send(tagged, 2 * far) for far in range(1, n_seq // 2)]
    chunks = plane_chunks(n_seq // 2)
    gathered = []
    for chunk in chunks:
        a = jnp.concatenate([planes[far][:half] for far in chunk], axis=0)
        b = jnp.concatenate([planes[far][half:] for far in chunk], axis=0)
        a = jnp.concatenate([a, x_link.send(a, 2)], axis=0)
        b = jnp.concatenate([b, y_link.send(b, 1)], axis=0)
        gathered.append(
            jnp.concatenate([a, y_link.send(a, 1), b, x_link.send(b, 2)], axis=0)
        )
    partials = []
    for tokens in gathered:
        table = tokens[:, depth:].astype(jnp.float32)
        lanes = jnp.arange(table.shape[1], dtype=jnp.int32)[None, :]
        partial = 0.0
        for m in range(2):
            mine = (lanes == ids[m]) | (lanes == ids[m] + experts)
            gate = jnp.sum(jnp.where(mine, table, 0.0), axis=1, keepdims=True)
            both = jnp.dot(tokens[:, :depth], in_weights[m], preferred_element_type=jnp.float32)
            act = (jax.nn.silu(both[:, :width]) * both[:, width:] * gate).astype(jnp.bfloat16)
            partial = partial + jnp.dot(act, out_weights[m], preferred_element_type=jnp.float32)
        partials.append(partial.astype(jnp.bfloat16))
    total = 0.0
    for at in list(range(1, len(chunks))) + [0]:
        chunk, partial = chunks[at], partials[at]
        part = len(chunk) * half
        a = added(partial[: 2 * part], y_link.send(partial[2 * part : 4 * part], 1))
        b = added(partial[4 * part : 6 * part], x_link.send(partial[6 * part :], 2))
        a = added(a[:part], x_link.send(a[part:], 2))
        b = added(b[:part], y_link.send(b[part:], 1))
        for place, far in enumerate(chunk):
            span = slice(place * half, (place + 1) * half)
            block = jnp.concatenate([a[span], b[span]], axis=0)
            if far > 0:
                block = z_link.send(block, 2 * far)
            total = total + block.astype(jnp.float32)
    return total


def experts_exchanged(ffn_in, router_weight, routes, expert_in, expert_out):
    tok_count = ffn_in.shape[0]
    experts = router_weight.shape[1]
    capacity = 2 * tok_count * TOPK // experts
    probs, chosen = router_gates(ffn_in, router_weight, routes)
    picked = jnp.sum(jnp.where(chosen, probs[:, None, :], 0.0), axis=-1)
    gates = picked / jnp.sum(picked, axis=-1, keepdims=True)
    flat_hot = chosen.reshape(tok_count * TOPK, experts).astype(jnp.int32)
    before = jnp.cumsum(flat_hot, axis=0) - flat_hot
    slots = jnp.sum(before * flat_hot, axis=-1).reshape(tok_count, TOPK)
    slot_hot = slots[:, :, None] == jnp.arange(capacity, dtype=jnp.int32)[None, None, :]
    placing = jnp.sum(
        (chosen[:, :, :, None] & slot_hot[:, :, None, :]).astype(jnp.bfloat16), axis=1
    )
    sending = jnp.einsum("tec,td->ecd", placing, ffn_in, preferred_element_type=jnp.float32).astype(
        jnp.bfloat16
    )
    received = lax.all_to_all(sending, ("exp", "seq"), split_axis=0, concat_axis=0, tiled=True)
    flat = received.reshape(-1, received.shape[-1])
    both = jnp.dot(flat, expert_in[0], preferred_element_type=jnp.float32)
    width = expert_out.shape[1]
    act = (jax.nn.silu(both[:, :width]) * both[:, width:]).astype(jnp.bfloat16)
    result = jnp.dot(act, expert_out[0], preferred_element_type=jnp.float32).astype(jnp.bfloat16)
    returned = lax.all_to_all(
        result.reshape(received.shape), ("exp", "seq"), split_axis=0, concat_axis=0, tiled=True
    )
    index = (routes * capacity + slots).reshape(-1)
    rows = jnp.take(returned.reshape(experts * capacity, -1), index, axis=0).reshape(
        tok_count, TOPK, -1
    )
    mixture = jnp.einsum("tk,tkd->td", gates, rows.astype(jnp.float32))
    return mixture


def local(
    hidden_in,
    doc_ids,
    attn_gain,
    q_weight,
    kv_weight,
    q_gain,
    k_gain,
    out_weight,
    ffn_gain,
    router_weight,
    routes,
    expert_in,
    expert_out,
    *,
    n_exp,
    n_seq,
):
    links = (Link("exp", n_exp), Link("exp", n_exp), Link("seq", n_seq), Link("seq", n_seq, 2))
    attn_rows = attention_rows(
        hidden_in, doc_ids, attn_gain, q_weight, kv_weight, q_gain, k_gain, out_weight, links
    )
    tok_count = hidden_in.shape[0]
    capacity = 2 * tok_count * TOPK // router_weight.shape[1]
    gathering = n_exp == 4 and 2 * capacity >= tok_count
    if gathering:
        in_weights = [expert_in[0], links[1].send(expert_in[0], 1)]
        out_weights = [expert_out[0], links[1].send(expert_out[0], 1)]
    mid = (hidden_in.astype(jnp.float32) + attn_rows).astype(jnp.bfloat16)
    ffn_in = rms_scale(mid.astype(jnp.float32), ffn_gain).astype(jnp.bfloat16)
    if gathering:
        mixture = experts_gathered(ffn_in, router_weight, routes, in_weights, out_weights, links)
    else:
        mixture = experts_exchanged(ffn_in, router_weight, routes, expert_in, expert_out)
    return (mid.astype(jnp.float32) + mixture).astype(jnp.bfloat16)


def solution(mesh):
    in_specs = (
        P(("exp", "seq"), None),
        P(("exp", "seq")),
        P(),
        P("exp", "seq"),
        P(None, "exp", None),
        P(),
        P(),
        P("seq", "exp"),
        P(),
        P(),
        P(("exp", "seq"), None),
        P(("exp", "seq"), None, None),
        P(("exp", "seq"), None, None),
    )
    out_specs = P(("exp", "seq"), None)
    body = functools.partial(local, n_exp=mesh.shape["exp"], n_seq=mesh.shape["seq"])
    return jax.shard_map(body, mesh=mesh, in_specs=in_specs, out_specs=out_specs, check_vma=False)
```
